512 devices in a mesh: expert: 64 (over z, y), tensor: 8 (over x, core).
Axes of the slice: x: 4, y: 4, z: 16, core: 2. Of those that a mesh axis runs over, the one named last changes fastest.
Arguments:
- tokens: bfloat16 [32768, 1024], P('expert', 'tensor'), may hold values from -6 to 6
- expert_ids: int32 [32768], P('expert'), may hold values from 0 to 63, as said below
- gate_scale: float32 [32768], P('expert'), may hold values from 0.25 to 1
- gate_weight: bfloat16 [64, 1024, 6144], P('expert', None, 'tensor'), may hold values from -0.1875 to 0.1875
- up_weight: bfloat16 [64, 1024, 6144], P('expert', None, 'tensor'), may hold values from -0.1875 to 0.1875
- down_weight: bfloat16 [64, 6144, 1024], P('expert', 'tensor'), may hold values from -0.109375 to 0.109375
Outputs:
- combined: bfloat16 [32768, 1024], P('expert', 'tensor')
The draws below stay inside these ranges and needn't reach their ends.
Inputs may be any that keep to these rules, and one draw needn't show every extreme that they name: `expert_ids`: among the 512 tokens of one index of expert, no expert id appears more than 16 times, and one expert, the same for every index, appears exactly 16 times in each.
All inputs are finite; a program needn't handle non-finite values.
Results may differ from the reference program's by a relative error of at most 0.02.
Values may be sent and summed in bfloat16 or wider, within the bound.
A program may use at most 64 MiB of HBM per device.

```python
import jax
import jax.numpy as jnp
from jax import lax

D = 1024
FF = 6144
TOK_DEV = 512
EXPERTS = 64
TOKENS = 32768
CAP = 16
SLOTS = 1024
HID_DEV = 768
N_TENSOR = 8


def draw_expert_ids(key, part):
    hot_key, rest_key = jax.random.split(key)
    hot = jax.random.randint(hot_key, (), 0, EXPERTS).astype(jnp.int32)

    def one_block(block_key):
        first_key, second_key = jax.random.split(block_key)
        chosen = jax.random.permutation(first_key, (EXPERTS - 1) * CAP)[:TOK_DEV - CAP]
        others = (chosen // CAP).astype(jnp.int32)
        others = others + (others >= hot).astype(jnp.int32)
        block_ids = jnp.concatenate([jnp.full((CAP,), hot, jnp.int32), others])
        return jax.random.permutation(second_key, block_ids)
    block_keys = jax.random.split(rest_key, TOKENS // TOK_DEV)
    return jax.vmap(one_block)(block_keys).reshape(TOKENS).astype(jnp.int32)


def with_spikes(drawn, stream_key, source, target, blocks, factor):
    owner, partner = [(jnp.arange(drawn.shape[dim]) // (drawn.shape[dim] // blocks)).reshape([-1 if axis == dim else 1 for axis in range(drawn.ndim)]) for dim in (source, target)]
    chosen = jax.random.permutation(stream_key, blocks)[partner]
    strong = (owner == chosen) | (owner == (partner + blocks // 2) % blocks)
    return jnp.where(strong, factor * drawn, drawn)


def levels(key, extent, shards, low, high):
    gain, own = 1.0, jax.random.fold_in(key, 6)
    for dim, parts in shards:
        steps = jnp.exp(jax.random.uniform(jax.random.fold_in(own, dim), (parts,), jnp.float32, low / len(shards), high / len(shards)))
        gain = gain * jnp.repeat(steps, extent[dim] // parts).reshape([-1 if axis == dim else 1 for axis in range(len(extent))])
    return gain


def bell_draw(stream_key, shape, width, reach, pieces=(), kind=jnp.bfloat16):
    values = width * jax.random.normal(stream_key, shape, jnp.float32)
    if pieces:
        values = values * levels(stream_key, shape, pieces, -0.22, 0.18)
    return jnp.clip(values, -reach, reach).astype(kind)


def heavy_noise(own_key, extent, deviation, most, cuts, heavy, kind=jnp.bfloat16):
    array = deviation * jax.random.normal(own_key, extent, jnp.float32)
    if cuts:
        array = array * levels(own_key, extent, cuts, -0.22, 0.18)
    return jnp.clip(with_spikes(array, jax.random.fold_in(own_key, 3), *heavy), -most, most).astype(kind)


def setup_inputs(seed: int = 0) -> dict:
    splits = jax.random.split(jax.random.key(seed), 7)
    return {
        "tokens": bell_draw(splits[0], (TOKENS, D), 1.0, 6.0, ((0, 64), (1, 8))),
        "expert_ids": draw_expert_ids(jax.random.fold_in(splits[6], 71), 0),
        "gate_scale": jnp.clip(0.25 + 0.75 * jax.random.uniform(splits[2], (TOKENS,), jnp.float32) ** levels(splits[2], (TOKENS,), ((0, 64),), -0.2, 0.2), 0.25, 1.0),
        "gate_weight": bell_draw(splits[3], (EXPERTS, D, FF), D ** -0.5, 0.1875, ((0, 64), (2, 8))),
        "up_weight": bell_draw(splits[4], (EXPERTS, D, FF), D ** -0.5, 0.1875, ((0, 64), (2, 8))),
        "down_weight": heavy_noise(splits[5], (EXPERTS, FF, D), FF ** -0.5, 0.109375, ((0, 64), (1, 8)), (1, 2, 8, 2.0)),
    }


def expert_rows(rows, w_gate, w_up, w_down):
    gate = jnp.dot(rows, w_gate, preferred_element_type=jnp.float32)
    up = jnp.dot(rows, w_up, preferred_element_type=jnp.float32)
    hidden = (jax.nn.silu(gate) * up).astype(jnp.bfloat16)
    hid_slices = hidden.astype(jnp.float32).reshape(rows.shape[0], N_TENSOR, HID_DEV)
    down_slices = w_down.astype(jnp.float32).reshape(N_TENSOR, HID_DEV, D)
    partials = jnp.einsum("rtf,tfd->trd", hid_slices, down_slices).astype(jnp.bfloat16)
    return jnp.sum(partials.astype(jnp.float32), axis=0).astype(jnp.bfloat16)


def reference(tokens, expert_ids, gate_scale, gate_weight, up_weight, down_weight):
    order = jnp.argsort(expert_ids, stable=True).astype(jnp.int32)
    sorted_ids = expert_ids[order]
    owners = jnp.arange(EXPERTS, dtype=jnp.int32)
    counts = jnp.sum((expert_ids[:, None] == owners[None, :]).astype(jnp.int32), axis=0)
    starts = (jnp.cumsum(counts) - counts).astype(jnp.int32)
    padded = jnp.concatenate([tokens[order], jnp.zeros((SLOTS, D), tokens.dtype)], axis=0)

    def one_expert(index):
        rows = lax.dynamic_slice_in_dim(padded, starts[index], SLOTS, 0)
        return expert_rows(rows, gate_weight[index], up_weight[index], down_weight[index])

    results = lax.map(one_expert, owners)
    position = jnp.arange(TOKENS, dtype=jnp.int32) - starts[sorted_ids]
    flat = results.reshape(EXPERTS * SLOTS, D)
    sorted_out = flat[(sorted_ids * SLOTS + position).astype(jnp.int32)]
    unsorted = jnp.zeros_like(sorted_out).at[order].set(sorted_out)
    return (gate_scale[:, None] * unsorted.astype(jnp.float32)).astype(jnp.bfloat16)
```

```python
import jax
import jax.numpy as jnp
from jax import lax
from jax.experimental import pallas as pl
from jax.experimental.pallas import tpu as pltpu
from jax.sharding import PartitionSpec as P

NZ, NY, NX, NC = 16, 4, 4, 2
CHUNKS, PER = 4, 4
CAP = 16
TOK = 512
D = 1024
FEAT = 128
WIDE = 256
HID = 768
ROWS = PER * 2 * CAP
DZ = (8, 0, 4, -4, 7, -6, -2, 1, -7, 6, 2, -1, 5, -5, 3, -3)
BF = jnp.bfloat16
F32 = jnp.float32


def dev(z, y, x, c):
    return {"expert": z * NY + y, "tensor": x * NC + c}


def rcopy(src, dst, send, recv, target):
    return pltpu.make_async_remote_copy(
        src_ref=src, dst_ref=dst, send_sem=send, recv_sem=recv,
        device_id=target, device_id_type=pl.DeviceIdType.MESH,
    )


def kernel(ids_ref, scale_ref, tok_ref, wg_hbm, wu_hbm, wd_hbm, out_ref,
           outg, mid, xbuf, ybuf, rsbuf, zbuf, mid2, ret, pick, scol, wg, wu, wd,
           w_sem, ws_send, ws_recv, y_send, y_self, y_recv, z_send, z_recv, ag_send, ag_recv,
           rs_send, rs_recv, zr_send, zr_recv, yr_send, yr_recv):
    e = lax.axis_index("expert")
    t = lax.axis_index("tensor")
    z, y, x, c = e // NY, e % NY, t // NC, t % NC
    half, within = y // 2, y % 2
    cols = pl.ds(pl.multiple_of(x * WIDE, WIDE), WIDE)
    my_cols = pl.ds(pl.multiple_of(c * FEAT, FEAT), FEAT)

    barrier = pltpu.get_barrier_semaphore()
    peers = [dev((z + d) % NZ, y, x, c) for d in (8, 7, 9, 6, 10, 5, 11, 4, 12, 3, 13, 2, 14, 1, 15)]
    peers += [dev(z, (y + d) % NY, x, cc) for d in (2, 1, 3) for cc in (0, 1)]
    peers += [dev(z, y, (x + d) % NX, c) for d in (2, 1, 3)] + [dev(z, y, x, 1 - c)]
    for peer in peers:
        pl.semaphore_signal(barrier, inc=1, device_id=peer, device_id_type=pl.DeviceIdType.MESH)

    weights = ((wg_hbm, wg), (wu_hbm, wu), (wd_hbm, wd))
    own = [pltpu.make_async_copy(hbm, buf.at[0], w_sem.at[n]) for n, (hbm, buf) in enumerate(weights)]
    for copy in own:
        copy.start()

    row = lax.broadcasted_iota(jnp.int32, (64, TOK), 0)
    place = (row >> 4) * PER + (row & 3)
    dz = jnp.zeros_like(row)
    for i, d in enumerate(DZ):
        dz = jnp.where(place == i, d, dz)
    owner = ((z - dz) & (NZ - 1)) * NY + ((row >> 2) & 3)
    hot = owner == ids_ref[...]
    before = (lax.broadcasted_iota(jnp.int32, (TOK, TOK), 0)
              < lax.broadcasted_iota(jnp.int32, (TOK, TOK), 1)).astype(F32).astype(BF)
    earlier = jnp.dot(hot.astype(F32).astype(BF), before, preferred_element_type=F32)
    slot = jnp.sum(jnp.where(hot, earlier + (row * CAP).astype(F32), 0.0), axis=0, keepdims=True)
    slot_i = slot.astype(jnp.int32)
    for k in range(CHUNKS):
        rows = lax.broadcasted_iota(jnp.int32, (256, TOK), 0) + k * 256
        sel = (rows == slot_i).astype(F32).astype(BF)
        part = jnp.dot(sel, tok_ref[...], preferred_element_type=F32).astype(BF)
        outg[k] = part.reshape(NY, PER, CAP, FEAT)

    pl.semaphore_wait(barrier, len(peers))

    def along_y(k):
        for d in (2, 1, 3):
            yy = (y + d) % NY
            rcopy(outg.at[k, yy], mid.at[pl.ds(k * PER, PER), within, :, my_cols],
                  y_send, y_recv.at[k], dev(z, yy, x, half)).start()
        src = outg.at[k, y]
        dst = mid.at[pl.ds(k * PER, PER), within, :, my_cols]

        @pl.when(c == half)
        def _():
            pltpu.make_async_copy(src, dst, y_recv.at[k]).start()

        @pl.when(c != half)
        def _():
            rcopy(src, dst, y_self, y_recv.at[k], dev(z, y, x, 1 - c)).start()

    for k in range(CHUNKS):
        along_y(k)
    sib = dev(z, y, x, 1 - c)
    swap = [rcopy(hbm, buf.at[1], ws_send.at[n], ws_recv.at[n], sib) for n, (hbm, buf) in enumerate(weights)]
    for copy in swap:
        copy.start()

    for k in range(CHUNKS):
        whole = mid.at[pl.ds(k * PER, PER)]
        pltpu.make_async_copy(whole, whole, y_recv.at[k]).wait()
        for i in range(k * PER, (k + 1) * PER):
            dst = xbuf.at[i, :, :, cols]
            if DZ[i] == 0:
                pltpu.make_async_copy(mid.at[i], dst, z_recv.at[k]).start()
            else:
                rcopy(mid.at[i], dst, z_send, z_recv.at[k], dev((z - DZ[i]) % NZ, y, x, c)).start()

    slot_col = jnp.broadcast_to(slot, (128, TOK)).T.astype(jnp.int32)
    scol[...] = jnp.broadcast_to(scale_ref[...], (128, TOK)).T
    for n in range(8):
        lanes = lax.broadcasted_iota(jnp.int32, (TOK, 128), 1) + n * 128
        pick[:, n * 128:(n + 1) * 128] = (lanes == slot_col).astype(F32).astype(BF)

    def gather(k):
        part = xbuf.at[pl.ds(k * PER, PER), :, :, cols]
        pltpu.make_async_copy(part, part, z_recv.at[k]).wait()
        for d in (2, 1, 3):
            rcopy(part, part, ag_send, ag_recv.at[k], dev(z, y, (x + d) % NX, c)).start()

    def ffn(k):
        three = xbuf.at[pl.ds(k * PER, PER), :, :, pl.ds(0, 3 * WIDE)]
        pltpu.make_async_copy(three, three, ag_recv.at[k]).wait()
        rows = xbuf[k * PER:(k + 1) * PER].reshape(ROWS, D)
        total = None
        for s in range(2):
            if k == 0:
                if s == 0:
                    for copy in own:
                        copy.wait()
                else:
                    for copy in swap:
                        copy.wait()
            gate = jnp.dot(rows, wg[s], preferred_element_type=F32)
            up = jnp.dot(rows, wu[s], preferred_element_type=F32)
            hidden = (gate / (1.0 + jnp.exp(-gate)) * up).astype(BF)
            part = jnp.dot(hidden, wd[s], preferred_element_type=F32)
            total = part if total is None else total + part
        total = total.astype(BF)
        for n in range(NX):
            ybuf[n, k] = total[:, n * WIDE:(n + 1) * WIDE]
        for d in (2, 1, 3):
            xx = (x + d) % NX
            rcopy(ybuf.at[xx, k], rsbuf.at[k, d - 1], rs_send, rs_recv.at[k], dev(z, y, xx, c)).start()

    def back_z(k):
        three = rsbuf.at[k]
        pltpu.make_async_copy(three, three, rs_recv.at[k]).wait()
        total = ybuf[x, k].astype(F32)
        for n in range(3):
            total += rsbuf[k, n].astype(F32)
        zbuf[k * PER:(k + 1) * PER] = total.astype(BF).reshape(PER, 2, CAP, WIDE)
        for i in range(k * PER, (k + 1) * PER):
            if DZ[i] == 0:
                pltpu.make_async_copy(zbuf.at[i], mid2.at[i], zr_recv.at[k]).start()
            else:
                rcopy(zbuf.at[i], mid2.at[i], zr_send, zr_recv.at[k], dev((z + DZ[i]) % NZ, y, x, c)).start()

    def back_y(k):
        whole = mid2.at[pl.ds(k * PER, PER)]
        pltpu.make_async_copy(whole, whole, zr_recv.at[k]).wait()
        for s in range(2):
            for cc in range(NC):
                src = mid2.at[pl.ds(k * PER, PER), s, :, pl.ds(cc * FEAT, FEAT)]
                yy = 2 * c + s
                mine = jnp.logical_and(yy == y, c == cc)

                @pl.when(mine)
                def _():
                    pltpu.make_async_copy(src, ret.at[k, y], yr_recv.at[k]).start()

                @pl.when(jnp.logical_not(mine))
                def _():
                    rcopy(src, ret.at[k, y], yr_send, yr_recv.at[k], dev(z, yy, x, cc)).start()

    def combine(k):
        whole = ret.at[k]
        pltpu.make_async_copy(whole, whole, yr_recv.at[k]).wait()
        return jnp.dot(pick[:, k * 256:(k + 1) * 256], ret[k].reshape(256, FEAT), preferred_element_type=F32)

    gather(0)
    gather(1)
    ffn(0)
    gather(2)
    ffn(1)
    back_z(0)
    gather(3)
    ffn(2)
    back_z(1)
    back_y(0)
    ffn(3)
    back_z(2)
    back_y(1)
    back_z(3)
    back_y(2)
    back_y(3)
    picked = combine(0)
    for k in range(1, CHUNKS):
        picked += combine(k)
    out_ref[...] = (scol[...] * picked).astype(BF)

    def sent(ref, sem):
        pltpu.make_async_copy(ref, ref, sem).wait()

    sent(outg.at[:, pl.ds(0, 3)], y_send)

    @pl.when(c != half)
    def _():
        sent(outg.at[:, 0], y_self)

    sent(mid.at[pl.ds(0, NZ - 1)], z_send)
    sent(xbuf.at[:, :, :, pl.ds(0, 3 * WIDE)], ag_send)
    sent(ybuf.at[pl.ds(0, 3)], rs_send)
    sent(zbuf.at[pl.ds(0, NZ - 1)], zr_send)

    @pl.when(c == half)
    def _():
        sent(ret.at[:, pl.ds(0, 3)], yr_send)

    @pl.when(c != half)
    def _():
        sent(ret, yr_send)


def shards(tokens, expert_ids, gate_scale, gate_weight, up_weight, down_weight):
    vmem = pl.BlockSpec(memory_space=pltpu.VMEM)
    hbm = pl.BlockSpec(memory_space=pl.ANY)
    dma = pltpu.SemaphoreType.DMA
    return pl.pallas_call(
        kernel,
        out_shape=jax.ShapeDtypeStruct((TOK, FEAT), BF),
        in_specs=[vmem, vmem, vmem, hbm, hbm, hbm],
        out_specs=vmem,
        scratch_shapes=[
            pltpu.VMEM((CHUNKS, NY, PER, CAP, FEAT), BF),
            pltpu.VMEM((NZ, 2, CAP, WIDE), BF),
            pltpu.VMEM((NZ, 2, CAP, D), BF),
            pltpu.VMEM((NX, CHUNKS, ROWS, WIDE), BF),
            pltpu.VMEM((CHUNKS, 3, ROWS, WIDE), BF),
            pltpu.VMEM((NZ, 2, CAP, WIDE), BF),
            pltpu.VMEM((NZ, 2, CAP, WIDE), BF),
            pltpu.VMEM((CHUNKS, NY, PER, CAP, FEAT), BF),
            pltpu.VMEM((TOK, CHUNKS * 256), BF),
            pltpu.VMEM((TOK, FEAT), F32),
            pltpu.VMEM((2, D, HID), BF),
            pltpu.VMEM((2, D, HID), BF),
            pltpu.VMEM((2, HID, D), BF),
            dma((3,)), dma((3,)), dma((3,)),
            dma, dma, dma((CHUNKS,)),
            dma, dma((CHUNKS,)),
            dma, dma((CHUNKS,)),
            dma, dma((CHUNKS,)),
            dma, dma((CHUNKS,)),
            dma, dma((CHUNKS,)),
        ],
        compiler_params=pltpu.CompilerParams(
            collective_id=0, has_side_effects=True, vmem_limit_bytes=56 << 20
        ),
        name="moe",
    )(expert_ids.reshape(1, TOK), gate_scale.reshape(1, TOK), tokens, gate_weight[0], up_weight[0], down_weight[0])


def solution(mesh):
    in_specs = (
        P("expert", "tensor"),
        P("expert"),
        P("expert"),
        P("expert", None, "tensor"),
        P("expert", None, "tensor"),
        P("expert", "tensor", None),
    )
    out_specs = P("expert", "tensor")
    return jax.shard_map(shards, mesh=mesh, in_specs=in_specs, out_specs=out_specs, check_vma=False)
```

```python
import jax
import jax.numpy as jnp
from jax import lax
from jax.experimental import pallas as pl
from jax.experimental.pallas import tpu as pltpu
from jax.sharding import PartitionSpec as P

NZ, NY, NX, NC = 16, 4, 4, 2
CHUNKS = 8
PER = 2
CAP = 16
TOK = 512
D = 1024
FEAT = 128
WIDE = 256
HID = 768
ROWS = PER * 2 * CAP
SLOTS = PER * NY * CAP
DZ = (8, 7, -7, 6, -6, 5, -5, 4, -4, 3, -3, 2, 0, 1, -1, -2)
ISSUE = tuple(range(CHUNKS))
BF = jnp.bfloat16
F32 = jnp.float32
MESH = pl.DeviceIdType.MESH


def wrap(a, n):
    return lax.rem(a, n)


def dev(z, y, x, c):
    return {"expert": z * NY + y, "tensor": x * NC + c}


def rcopy(src, dst, send, recv, target):
    return pltpu.make_async_remote_copy(
        src_ref=src, dst_ref=dst, send_sem=send, recv_sem=recv, device_id=target, device_id_type=MESH
    )


def done(ref, sem):
    pltpu.make_async_copy(ref, ref, sem).wait()


def kernel(ids_ref, tok_ref, wg_hbm, wu_hbm, wd_hbm, out_ref,
           outg, arr, xbuf, ybuf, rsbuf, zbuf, ret, pick, wg, wu, wd,
           w_sem, ws_send, ws_recv, d_send, d_recv, ag_send, ag_recv, rs_send, rs_recv, rt_send, rt_recv):
    e = lax.axis_index("expert")
    t = lax.axis_index("tensor")
    z, y = lax.div(e, NY), lax.rem(e, NY)
    x, c = lax.div(t, NC), lax.rem(t, NC)
    o = 1 - c
    right, left, far = wrap(x + 1, NX), wrap(x + 3, NX), wrap(x + 2, NX)
    ys = [y] + [wrap(y + d, NY) for d in (1, 2, 3)]

    def at_z(d):
        return wrap(z + (d + NZ), NZ) if d else z

    my_cols = pl.ds(pl.multiple_of(t * FEAT, FEAT), FEAT)

    barrier = pltpu.get_barrier_semaphore()
    peers = [(dz, dy) for dz in (8, 7, -7, 6, -6, 5, -5, 4, -4, 3, -3, 2, -2, 1, -1, 0) for dy in range(4)]
    peers = [dev(at_z(dz), ys[dy], x, c) for dz, dy in peers if (dz, dy) != (0, 0)]
    peers += [dev(z, y, xx, cc) for xx in (far, right, left) for cc in (0, 1)] + [dev(z, y, x, o)]
    for peer in peers:
        pl.semaphore_signal(barrier, inc=1, device_id=peer, device_id_type=MESH)

    weights = ((wg_hbm, wg), (wu_hbm, wu), (wd_hbm, wd))
    own = [pltpu.make_async_copy(hbm, buf.at[0], w_sem.at[n]) for n, (hbm, buf) in enumerate(weights)]
    for copy in own:
        copy.start()

    row = lax.broadcasted_iota(jnp.int32, (64, 128), 0)
    dz = jnp.zeros_like(row)
    for i, d in enumerate(DZ):
        dz = jnp.where((row >> 2) == i, d, dz)
    owner = ((z - dz) & (NZ - 1)) * NY + (row & 3)
    hot = jnp.concatenate([owner] * 4, axis=1) == ids_ref[...]
    before = (lax.broadcasted_iota(jnp.int32, (TOK, TOK), 0)
              < lax.broadcasted_iota(jnp.int32, (TOK, TOK), 1)).astype(F32).astype(BF)
    earlier = jnp.dot(hot.astype(F32).astype(BF), before, preferred_element_type=F32)
    base = lax.broadcasted_iota(jnp.int32, (64, TOK), 0).astype(F32) * float(CAP)
    slot = jnp.sum(jnp.where(hot, earlier + base, 0.0), axis=0, keepdims=True)
    slot_i = slot.astype(jnp.int32)
    for k in range(CHUNKS):
        rows = lax.broadcasted_iota(jnp.int32, (SLOTS, TOK), 0) + k * SLOTS
        sel = (rows == slot_i).astype(F32).astype(BF)
        part = jnp.dot(sel, tok_ref[...], preferred_element_type=F32).astype(BF)
        outg[k * PER:(k + 1) * PER] = part.reshape(PER, NY, CAP, FEAT)

    pl.semaphore_wait(barrier, len(peers))

    for k in ISSUE:
        for i in range(k * PER, (k + 1) * PER):
            for n, yy in enumerate(ys):
                if DZ[i] == 0 and n == 0:
                    pltpu.make_async_copy(outg.at[i, yy], arr.at[i, y], d_recv.at[k]).start()
                else:
                    rcopy(outg.at[i, yy], arr.at[i, y], d_send, d_recv.at[k], dev(at_z(-DZ[i]), yy, x, c)).start()
    sib = dev(z, y, x, o)
    swap = [rcopy(hbm, buf.at[1], ws_send.at[n], ws_recv.at[n], sib) for n, (hbm, buf) in enumerate(weights)]
    for copy in swap:
        copy.start()

    slot_col = jnp.broadcast_to(slot, (128, TOK)).T.astype(jnp.int32)
    for n in range(8):
        lanes = lax.broadcasted_iota(jnp.int32, (TOK, 128), 1) + n * 128
        pick[:, n * 128:(n + 1) * 128] = (lanes == slot_col).astype(F32).astype(BF)

    def places(k):
        return pl.ds(k * PER, PER)

    def gather(k):
        done(arr.at[places(k)], d_recv.at[k])
        for xx in (far, right, left):
            for h in range(2):
                rcopy(arr.at[places(k), pl.ds(2 * h, 2)], xbuf.at[places(k), :, :, my_cols],
                      ag_send.at[k], ag_recv.at[k], dev(z, y, xx, h)).start()
        rcopy(arr.at[places(k), pl.ds(2 * o, 2)], xbuf.at[places(k), :, :, my_cols],
              ag_send.at[k], ag_recv.at[k], sib).start()
        pltpu.make_async_copy(arr.at[places(k), pl.ds(2 * c, 2)], xbuf.at[places(k), :, :, my_cols],
                              ag_recv.at[k]).start()

    def ffn(k):
        done(xbuf.at[places(k)], ag_recv.at[k])
        rows = xbuf[k * PER:(k + 1) * PER].reshape(ROWS, D)
        total = None
        for s in range(2):
            if k == 0:
                for copy in (own, swap)[s]:
                    copy.wait()
            gate = jnp.dot(rows, wg[s], preferred_element_type=F32)
            up = jnp.dot(rows, wu[s], preferred_element_type=F32)
            hidden = (gate / (1.0 + jnp.exp(-gate)) * up).astype(BF)
            part = jnp.dot(hidden, wd[s], preferred_element_type=F32)
            total = part if total is None else total + part
        total = total.astype(BF)
        for n in range(NX * NC):
            ybuf[n, k] = total[:, n * FEAT:(n + 1) * FEAT]
        for side, target in enumerate((right, left, far)):
            for cc in range(NC):
                rcopy(ybuf.at[NC * target + cc, k], rsbuf.at[k, 4 * c + side],
                      rs_send.at[k], rs_recv.at[k], dev(z, y, target, cc)).start()
        rcopy(ybuf.at[NC * x + o, k], rsbuf.at[k, 4 * c + 3], rs_send.at[k], rs_recv.at[k], sib).start()
        rsbuf[k, 4 * c + 3] = ybuf[t, k]

    def back(k):
        done(rsbuf.at[k, pl.ds(0, 7)], rs_recv.at[k])
        for h in range(2):
            total = rsbuf[k, 4 * h + 3].astype(F32)
            for n in range(3):
                total += rsbuf[k, 4 * h + n].astype(F32)
            zbuf[k * PER:(k + 1) * PER, 2 * h:2 * h + 2] = total.astype(BF).reshape(PER, 2, CAP, FEAT)
        for i in range(k * PER, (k + 1) * PER):
            for n, yy in enumerate(ys):
                if DZ[i] == 0 and n == 0:
                    pltpu.make_async_copy(zbuf.at[i, yy], ret.at[i, y], rt_recv.at[k]).start()
                else:
                    rcopy(zbuf.at[i, yy], ret.at[i, y], rt_send, rt_recv.at[k], dev(at_z(DZ[i]), yy, x, c)).start()

    def combine(k):
        done(ret.at[places(k)], rt_recv.at[k])
        return jnp.dot(pick[:, k * SLOTS:(k + 1) * SLOTS], ret[k * PER:(k + 1) * PER].reshape(SLOTS, FEAT),
                       preferred_element_type=F32)

    gather(0)
    gather(1)
    gather(2)
    gather(3)
    ffn(0)
    gather(4)
    ffn(1)
    gather(5)
    ffn(2)
    gather(6)
    ffn(3)
    back(0)
    gather(7)
    ffn(4)
    back(1)
    ffn(5)
    back(2)
    ffn(6)
    back(3)
    ffn(7)
    back(4)
    back(5)
    back(6)
    back(7)
    picked = combine(0)
    for k in range(1, CHUNKS):
        picked += combine(k)
    out_ref[...] = picked.astype(BF)

    blocks = wg.at[0, pl.ds(0, 63 * CAP), pl.ds(0, FEAT)]
    done(blocks, d_send)
    for k in range(CHUNKS):
        done(rsbuf.at[k, pl.ds(0, 7)], ag_send.at[k])
        done(rsbuf.at[k, pl.ds(0, 7)], rs_send.at[k])
    done(blocks, rt_send)


def shards(tokens, expert_ids, gate_scale, gate_weight, up_weight, down_weight):
    vmem = pl.BlockSpec(memory_space=pltpu.VMEM)
    hbm = pl.BlockSpec(memory_space=pl.ANY)
    dma = pltpu.SemaphoreType.DMA
    picked = pl.pallas_call(
        kernel,
        out_shape=jax.ShapeDtypeStruct((TOK, FEAT), BF),
        in_specs=[vmem, vmem, hbm, hbm, hbm],
        out_specs=vmem,
        scratch_shapes=[
            pltpu.VMEM((NZ, NY, CAP, FEAT), BF),
            pltpu.VMEM((NZ, NY, CAP, FEAT), BF),
            pltpu.VMEM((NZ, 2, CAP, D), BF),
            pltpu.VMEM((NX * NC, CHUNKS, ROWS, FEAT), BF),
            pltpu.VMEM((CHUNKS, 8, ROWS, FEAT), BF),
            pltpu.VMEM((NZ, NY, CAP, FEAT), BF),
            pltpu.VMEM((NZ, NY, CAP, FEAT), BF),
            pltpu.VMEM((TOK, CHUNKS * SLOTS), BF),
            pltpu.VMEM((2, D, HID), BF),
            pltpu.VMEM((2, D, HID), BF),
            pltpu.VMEM((2, HID, D), BF),
            dma((3,)), dma((3,)), dma((3,)),
            dma, dma((CHUNKS,)),
            dma((CHUNKS,)), dma((CHUNKS,)),
            dma((CHUNKS,)), dma((CHUNKS,)),
            dma, dma((CHUNKS,)),
        ],
        compiler_params=pltpu.CompilerParams(
            collective_id=0, has_side_effects=True, vmem_limit_bytes=56 << 20
        ),
        name="moe",
    )(expert_ids.reshape(1, TOK), tokens, gate_weight[0], up_weight[0], down_weight[0])
    return (gate_scale[:, None] * picked.astype(F32)).astype(BF)


def solution(mesh):
    in_specs = (
        P("expert", "tensor"),
        P("expert"),
        P("expert"),
        P("expert", None, "tensor"),
        P("expert", None, "tensor"),
        P("expert", "tensor", None),
    )
    out_specs = P("expert", "tensor")
    return jax.shard_map(shards, mesh=mesh, in_specs=in_specs, out_specs=out_specs, check_vma=False)
```

```python
import jax
import jax.numpy as jnp
from jax import lax
from jax.experimental import pallas as pl
from jax.experimental.pallas import tpu as pltpu
from jax.sharding import PartitionSpec as P

NZ, NY, NX, NC = 16, 4, 4, 2
CHUNKS = 8
PER = 2
CAP = 16
TOK = 512
D = 1024
FEAT = 128
WIDE = 256
HID = 768
ROWS = PER * 2 * CAP
SLOTS = PER * NY * CAP
DZ = (8, 0, 7, -7, 6, -6, 5, -5, 4, -4, 3, -3, 2, -2, 1, -1)
ISSUE = tuple(range(CHUNKS))
BF = jnp.bfloat16
F32 = jnp.float32
MESH = pl.DeviceIdType.MESH


def wrap(a, n):
    return lax.rem(a, n)


def dev(z, y, x, c):
    return {"expert": z * NY + y, "tensor": x * NC + c}


def rcopy(src, dst, send, recv, target):
    return pltpu.make_async_remote_copy(
        src_ref=src, dst_ref=dst, send_sem=send, recv_sem=recv, device_id=target, device_id_type=MESH
    )


def done(ref, sem):
    pltpu.make_async_copy(ref, ref, sem).wait()


def kernel(ids_ref, tok_ref, wg_hbm, wu_hbm, wd_hbm, out_ref,
           outg, arr, xbuf, ybuf, rsbuf, zbuf, ret, pick, wg, wu, wd,
           w_sem, ws_send, ws_recv, d_send, d_recv, ag_send, ag_recv, rs_send, rs_recv, rt_send, rt_recv):
    e = lax.axis_index("expert")
    t = lax.axis_index("tensor")
    z, y = lax.div(e, NY), lax.rem(e, NY)
    x, c = lax.div(t, NC), lax.rem(t, NC)
    o = 1 - c
    right, left, far = wrap(x + 1, NX), wrap(x + 3, NX), wrap(x + 2, NX)
    ys = [y] + [wrap(y + d, NY) for d in (2, 1, 3)]

    def at_z(d):
        return wrap(z + (d + NZ), NZ) if d else z

    my_cols = pl.ds(pl.multiple_of(t * FEAT, FEAT), FEAT)

    barrier = pltpu.get_barrier_semaphore()
    peers = [(dz, dy) for dz in (8, 7, -7, 6, -6, 5, -5, 4, -4, 3, -3, 2, -2, 1, -1, 0) for dy in range(4)]
    peers = [dev(at_z(dz), ys[dy], x, c) for dz, dy in peers if (dz, dy) != (0, 0)]
    peers += [dev(z, y, xx, cc) for xx in (far, right, left) for cc in (0, 1)] + [dev(z, y, x, o)]
    for peer in peers:
        pl.semaphore_signal(barrier, inc=1, device_id=peer, device_id_type=MESH)

    weights = ((wg_hbm, wg), (wu_hbm, wu), (wd_hbm, wd))
    own = [pltpu.make_async_copy(hbm, buf.at[0], w_sem.at[n]) for n, (hbm, buf) in enumerate(weights)]
    for copy in own:
        copy.start()

    row = lax.broadcasted_iota(jnp.int32, (64, 128), 0)
    dz = jnp.zeros_like(row)
    for i, d in enumerate(DZ):
        dz = jnp.where((row >> 2) == i, d, dz)
    owner = ((z - dz) & (NZ - 1)) * NY + (row & 3)
    hot = jnp.concatenate([owner] * 4, axis=1) == ids_ref[...]
    before = (lax.broadcasted_iota(jnp.int32, (TOK, TOK), 0)
              < lax.broadcasted_iota(jnp.int32, (TOK, TOK), 1)).astype(F32).astype(BF)
    earlier = jnp.dot(hot.astype(F32).astype(BF), before, preferred_element_type=F32)
    base = lax.broadcasted_iota(jnp.int32, (64, TOK), 0).astype(F32) * float(CAP)
    slot = jnp.sum(jnp.where(hot, earlier + base, 0.0), axis=0, keepdims=True)
    slot_i = slot.astype(jnp.int32)
    for k in range(CHUNKS):
        rows = lax.broadcasted_iota(jnp.int32, (SLOTS, TOK), 0) + k * SLOTS
        sel = (rows == slot_i).astype(F32).astype(BF)
        part = jnp.dot(sel, tok_ref[...], preferred_element_type=F32).astype(BF)
        outg[k * PER:(k + 1) * PER] = part.reshape(PER, NY, CAP, FEAT)

    pl.semaphore_wait(barrier, len(peers))

    sib = dev(z, y, x, o)
    swap = [rcopy(hbm, buf.at[1], ws_send.at[n], ws_recv.at[n], sib) for n, (hbm, buf) in enumerate(weights)]
    for copy in swap:
        copy.start()

    for k in ISSUE:
        for i in range(k * PER, (k + 1) * PER):
            for n, yy in enumerate(ys):
                if DZ[i] == 0 and n == 0:
                    pltpu.make_async_copy(outg.at[i, yy], arr.at[i, y], d_recv.at[k]).start()
                else:
                    rcopy(outg.at[i, yy], arr.at[i, y], d_send, d_recv.at[k], dev(at_z(-DZ[i]), yy, x, c)).start()
    slot_col = jnp.broadcast_to(slot, (128, TOK)).T.astype(jnp.int32)
    for n in range(8):
        lanes = lax.broadcasted_iota(jnp.int32, (TOK, 128), 1) + n * 128
        pick[:, n * 128:(n + 1) * 128] = (lanes == slot_col).astype(F32).astype(BF)

    def places(k):
        return pl.ds(k * PER, PER)

    def gather(k):
        done(arr.at[places(k)], d_recv.at[k])
        for xx in (far, right, left):
            for h in range(2):
                rcopy(arr.at[places(k), pl.ds(2 * h, 2)], xbuf.at[places(k), :, :, my_cols],
                      ag_send.at[k], ag_recv.at[k], dev(z, y, xx, h)).start()
        rcopy(arr.at[places(k), pl.ds(2 * o, 2)], xbuf.at[places(k), :, :, my_cols],
              ag_send.at[k], ag_recv.at[k], sib).start()
        pltpu.make_async_copy(arr.at[places(k), pl.ds(2 * c, 2)], xbuf.at[places(k), :, :, my_cols],
                              ag_recv.at[k]).start()

    def ffn(k):
        done(xbuf.at[places(k)], ag_recv.at[k])
        rows = xbuf[k * PER:(k + 1) * PER].reshape(ROWS, D)
        total = None
        for s in range(2):
            if k == 0:
                for copy in (own, swap)[s]:
                    copy.wait()
            gate = jnp.dot(rows, wg[s], preferred_element_type=F32)
            up = jnp.dot(rows, wu[s], preferred_element_type=F32)
            hidden = (gate / (1.0 + jnp.exp(-gate)) * up).astype(BF)
            part = jnp.dot(hidden, wd[s], preferred_element_type=F32)
            total = part if total is None else total + part
        total = total.astype(BF)
        for n in range(NX * NC):
            ybuf[n, k] = total[:, n * FEAT:(n + 1) * FEAT]
        for side, target in ((2, far), (0, right), (1, left)):
            for cc in range(NC):
                rcopy(ybuf.at[NC * target + cc, k], rsbuf.at[k, 4 * c + side],
                      rs_send.at[k], rs_recv.at[k], dev(z, y, target, cc)).start()
        rcopy(ybuf.at[NC * x + o, k], rsbuf.at[k, 4 * c + 3], rs_send.at[k], rs_recv.at[k], sib).start()
        rsbuf[k, 4 * c + 3] = ybuf[t, k]

    def back(k):
        done(rsbuf.at[k, pl.ds(0, 7)], rs_recv.at[k])
        for h in range(2):
            total = rsbuf[k, 4 * h + 3].astype(F32)
            for n in range(3):
                total += rsbuf[k, 4 * h + n].astype(F32)
            zbuf[k * PER:(k + 1) * PER, 2 * h:2 * h + 2] = total.astype(BF).reshape(PER, 2, CAP, FEAT)
        for i in range(k * PER, (k + 1) * PER):
            for n, yy in enumerate(ys):
                if DZ[i] == 0 and n == 0:
                    pltpu.make_async_copy(zbuf.at[i, yy], ret.at[i, y], rt_recv.at[k]).start()
                else:
                    rcopy(zbuf.at[i, yy], ret.at[i, y], rt_send, rt_recv.at[k], dev(at_z(DZ[i]), yy, x, c)).start()

    def combine(k):
        done(ret.at[places(k)], rt_recv.at[k])
        return jnp.dot(pick[:, k * SLOTS:(k + 1) * SLOTS], ret[k * PER:(k + 1) * PER].reshape(SLOTS, FEAT),
                       preferred_element_type=F32)

    gather(0)
    gather(1)
    gather(2)
    gather(3)
    ffn(0)
    gather(4)
    ffn(1)
    gather(5)
    ffn(2)
    gather(6)
    ffn(3)
    back(0)
    gather(7)
    ffn(4)
    back(1)
    ffn(5)
    back(2)
    ffn(6)
    back(3)
    ffn(7)
    back(4)
    back(5)
    back(6)
    back(7)
    picked = combine(0)
    for k in range(1, CHUNKS):
        picked += combine(k)
    out_ref[...] = picked.astype(BF)

    blocks = wg.at[0, pl.ds(0, 63 * CAP), pl.ds(0, FEAT)]
    done(blocks, d_send)
    for k in range(CHUNKS):
        done(rsbuf.at[k, pl.ds(0, 7)], ag_send.at[k])
        done(rsbuf.at[k, pl.ds(0, 7)], rs_send.at[k])
    done(blocks, rt_send)


def shards(tokens, expert_ids, gate_scale, gate_weight, up_weight, down_weight):
    vmem = pl.BlockSpec(memory_space=pltpu.VMEM)
    hbm = pl.BlockSpec(memory_space=pl.ANY)
    dma = pltpu.SemaphoreType.DMA
    picked = pl.pallas_call(
        kernel,
        out_shape=jax.ShapeDtypeStruct((TOK, FEAT), BF),
        in_specs=[vmem, vmem, hbm, hbm, hbm],
        out_specs=vmem,
        scratch_shapes=[
            pltpu.VMEM((NZ, NY, CAP, FEAT), BF),
            pltpu.VMEM((NZ, NY, CAP, FEAT), BF),
            pltpu.VMEM((NZ, 2, CAP, D), BF),
            pltpu.VMEM((NX * NC, CHUNKS, ROWS, FEAT), BF),
            pltpu.VMEM((CHUNKS, 8, ROWS, FEAT), BF),
            pltpu.VMEM((NZ, NY, CAP, FEAT), BF),
            pltpu.VMEM((NZ, NY, CAP, FEAT), BF),
            pltpu.VMEM((TOK, CHUNKS * SLOTS), BF),
            pltpu.VMEM((2, D, HID), BF),
            pltpu.VMEM((2, D, HID), BF),
            pltpu.VMEM((2, HID, D), BF),
            dma((3,)), dma((3,)), dma((3,)),
            dma, dma((CHUNKS,)),
            dma((CHUNKS,)), dma((CHUNKS,)),
            dma((CHUNKS,)), dma((CHUNKS,)),
            dma, dma((CHUNKS,)),
        ],
        compiler_params=pltpu.CompilerParams(
            collective_id=0, has_side_effects=True, vmem_limit_bytes=56 << 20
        ),
        name="moe",
    )(expert_ids.reshape(1, TOK), tokens, gate_weight[0], up_weight[0], down_weight[0])
    return (gate_scale[:, None] * picked.astype(F32)).astype(BF)


def solution(mesh):
    in_specs = (
        P("expert", "tensor"),
        P("expert"),
        P("expert"),
        P("expert", None, "tensor"),
        P("expert", None, "tensor"),
        P("expert", "tensor", None),
    )
    out_specs = P("expert", "tensor")
    return jax.shard_map(shards, mesh=mesh, in_specs=in_specs, out_specs=out_specs, check_vma=False)
```
